512 devices in a mesh: row: 16 (over z, x_lo), col: 32 (over x_hi, y, core).
Axes of the slice: x: 4 (x_hi: 2, x_lo: 2; x = x_hi * 2 + x_lo), y: 8, z: 8, core: 2. Of those that a mesh axis runs over, the one named last changes fastest.
Arguments:
- tokens: bfloat16 [2048, 4096], P('row', 'col'), may hold values from -6 to 6
- upstream: bfloat16 [2048, 4096], P('row', 'col'), may hold values from -6 to 6
- w_in: bfloat16 [32, 16, 256, 256], P('col', 'row'), may hold values from -0.1875 to 0.1875
- in_codes: int32 [32, 16], P('col'), may hold values from -1 to 31, as said below
- w_out: bfloat16 [32, 16, 256, 256], P('col', 'row'), may hold values from -0.09375 to 0.09375
- out_codes: int32 [32, 16], P('col'), may hold values from -1 to 31, as said below
Outputs:
- layer_out: bfloat16 [2048, 4096], P('row', 'col')
- grad_tokens: bfloat16 [2048, 4096], P('row', 'col')
- grad_w_in: bfloat16 [32, 16, 256, 256], P('col', 'row')
- grad_w_out: bfloat16 [32, 16, 256, 256], P('col', 'row')
The draws below stay inside these ranges and needn't reach their ends.
Inputs may be any that keep to these rules, and one draw needn't show every extreme that they name: `in_codes`: row c describes panel c's 16 slots: a code k names input tile row k // 2 and local hidden tile column k % 2; -1 marks an empty slot. Codes of a row are distinct, every row has one filled slot or more, and some row has all 16 slots filled. `out_codes`: row c describes panel c's 16 slots: a code k names output tile column k // 2 and local hidden tile row k % 2; -1 marks an empty slot. Codes of a row are distinct, every row has one filled slot or more, and some row has all 16 slots filled.
All inputs are finite; a program needn't handle non-finite values.
Results may differ from the reference program's by a relative error of at most 0.015.
Values may be sent and summed in bfloat16 or wider, within the bound.
A program may use at most 64 MiB of HBM per device.

```python
import jax
import jax.numpy as jnp
from jax import lax

D = 4096
FF = 16384
TILE = 256
TOKENS = 2048
PANELS = 32
CAP = 16


def draw_codes(key, salt_value):
    base_key = jax.random.fold_in(key, salt_value)
    tiles_all = D // TILE * (FF // (TILE * PANELS))
    full_panel = jax.random.randint(jax.random.fold_in(base_key, 1), (), 0, PANELS)

    def one_panel(panel_id):
        panel_key = jax.random.fold_in(base_key, panel_id + 7)
        chosen = jax.random.permutation(jax.random.fold_in(panel_key, 1), tiles_all)[:CAP].astype(jnp.int32)
        slot_rank = jax.random.permutation(jax.random.fold_in(panel_key, 2), CAP).astype(jnp.int32)
        filled = jax.random.randint(jax.random.fold_in(panel_key, 3), (), 1, CAP + 1)
        is_full = panel_id == full_panel
        filled = jnp.where(is_full, CAP, filled)
        shifted = (chosen + (tiles_all - 1 - chosen[0])) % tiles_all
        chosen = jnp.where(is_full, shifted, chosen)
        return jnp.where(slot_rank < filled, chosen, -1).astype(jnp.int32)
    return jax.vmap(one_panel)(jnp.arange(PANELS, dtype=jnp.int32))


def draw_in_codes(key, part):
    return draw_codes(key, 11)


def draw_out_codes(key, part):
    return draw_codes(key, 23)


def levels(key, extent, shards, smallest, high):
    level, own = 1.0, jax.random.fold_in(key, 6)
    for axis_at, blocks in shards:
        draws = jnp.exp(jax.random.uniform(jax.random.fold_in(own, axis_at), (blocks,), jnp.float32, smallest / len(shards), high / len(shards)))
        level = level * jnp.repeat(draws, extent[axis_at] // blocks).reshape([-1 if axis == axis_at else 1 for axis in range(len(extent))])
    return level


def gaussian(stream_key, shape, deviation, bound, cuts=(), held_as=jnp.bfloat16):
    gain = levels(stream_key, shape, cuts, -0.22, 0.18) if cuts else 1.0
    values = jax.random.normal(stream_key, shape, jnp.float32) * deviation * gain
    return jnp.minimum(jnp.maximum(values, -bound), bound).astype(held_as)


def setup_inputs(seed: int = 0) -> dict:
    seeds = jax.random.split(jax.random.key(seed), 7)
    tokens = gaussian(seeds[0], (TOKENS, D), 1.0, 6.0, ((0, 16), (1, 32)))
    upstream = gaussian(seeds[1], (TOKENS, D), 1.0, 6.0, ((0, 16), (1, 32)))
    w_in = gaussian(seeds[2], (PANELS, CAP, TILE, TILE), (D // 4) ** -0.5, 0.1875, ((0, 32), (1, 16)))
    in_codes = draw_in_codes(jax.random.fold_in(seeds[6], 71), 0)
    w_out = gaussian(seeds[4], (PANELS, CAP, TILE, TILE), (FF // 4) ** -0.5, 0.09375, ((0, 32), (1, 16)))
    out_codes = draw_out_codes(jax.random.fold_in(seeds[6], 71), 0)
    return {"tokens": tokens, "upstream": upstream, "w_in": w_in, "in_codes": in_codes, "w_out": w_out, "out_codes": out_codes}


def silu_slope(hidden):
    sigmoid_value = jax.nn.sigmoid(hidden)
    return sigmoid_value * (1.0 + hidden * (1.0 - sigmoid_value))


def split_codes(slot_codes, tile_cols):
    filled = slot_codes >= 0
    clipped = jnp.maximum(slot_codes, 0)
    return (clipped // tile_cols).astype(jnp.int32), (clipped % tile_cols).astype(jnp.int32), filled


def selector(position, filled, classes):
    matches = position[:, None] == jnp.arange(classes, dtype=jnp.int32)[None, :]
    return (matches & filled[:, None]).astype(jnp.float32)


def reference(tokens, upstream, w_in, in_codes, w_out, out_codes):
    tile_rows = D // TILE
    tile_cols = FF // (TILE * PANELS)
    token_tiles = tokens.reshape(TOKENS, tile_rows, TILE)
    up_tiles = upstream.reshape(TOKENS, tile_rows, TILE)
    highest = lax.Precision.HIGHEST

    def panel_step(carry, panel_data):
        layer_total, input_total = carry
        codes_in, tiles_in, codes_out, tiles_out = panel_data
        in_row, in_col, in_filled = split_codes(codes_in, tile_cols)
        out_row, out_col, out_filled = split_codes(codes_out, tile_cols)
        tiles_in32 = tiles_in.astype(jnp.float32)
        tiles_out32 = tiles_out.astype(jnp.float32)
        picked_tokens = jnp.take(token_tiles, in_row, axis=1).astype(jnp.float32)
        products = jnp.einsum('tkd,kdn->tkn', picked_tokens, tiles_in32)
        hidden = jnp.einsum('tkn,kj->tjn', products, selector(in_col, in_filled, tile_cols), precision=highest)
        activ = jax.nn.silu(hidden).astype(jnp.bfloat16)
        picked_activ = jnp.take(activ, out_col, axis=1).astype(jnp.float32)
        out_products = jnp.einsum('tkf,kfd->tkd', picked_activ, tiles_out32)
        layer_part = jnp.einsum('tkd,ki->tid', out_products, selector(out_row, out_filled, tile_rows), precision=highest)
        layer_part = lax.optimization_barrier(layer_part.reshape(TOKENS, D).astype(jnp.bfloat16)).astype(jnp.float32)
        picked_up = jnp.take(up_tiles, out_row, axis=1).astype(jnp.float32)
        back_products = jnp.einsum('tkd,kfd->tkf', picked_up, tiles_out32)
        grad_activ = jnp.einsum('tkf,kj->tjf', back_products, selector(out_col, out_filled, tile_cols), precision=highest)
        grad_hidden = (grad_activ * silu_slope(hidden)).astype(jnp.bfloat16)
        picked_grad = jnp.take(grad_hidden, in_col, axis=1).astype(jnp.float32)
        in_products = jnp.einsum('tkf,kdf->tkd', picked_grad, tiles_in32)
        input_part = jnp.einsum('tkd,ki->tid', in_products, selector(in_row, in_filled, tile_rows), precision=highest)
        input_part = lax.optimization_barrier(input_part.reshape(TOKENS, D).astype(jnp.bfloat16)).astype(jnp.float32)
        grad_in = jnp.einsum('tkd,tkn->kdn', picked_tokens, picked_grad)
        grad_in = jnp.where(in_filled[:, None, None], grad_in, 0.0).astype(jnp.bfloat16)
        grad_out = jnp.einsum('tkf,tkd->kfd', picked_activ, picked_up)
        grad_out = jnp.where(out_filled[:, None, None], grad_out, 0.0).astype(jnp.bfloat16)
        return (layer_total + layer_part, input_total + input_part), (grad_in, grad_out)

    zeros = jnp.zeros((TOKENS, D), jnp.float32)
    totals, grads = lax.scan(panel_step, (zeros, zeros), (in_codes, w_in, out_codes, w_out))
    return totals[0].astype(jnp.bfloat16), totals[1].astype(jnp.bfloat16), grads[0], grads[1]
```

```python
import jax
import jax.numpy as jnp
from jax import lax
from jax.sharding import PartitionSpec as P

D = 4096
FF = 16384


def silu_slope(hidden):
    sigmoid_value = jax.nn.sigmoid(hidden)
    return sigmoid_value * (1.0 + hidden * (1.0 - sigmoid_value))


def split_codes(slot_codes, tile_cols):
    filled = slot_codes >= 0
    clipped = jnp.maximum(slot_codes, 0)
    return (clipped // tile_cols, clipped % tile_cols, filled)


def selector(position, filled, classes):
    matches = position[:, None] == jnp.arange(classes, dtype=jnp.int32)[None, :]
    return matches & filled[:, None]


def exchange(blocks, axis):
    return lax.all_to_all(blocks, axis, split_axis=0, concat_axis=0, tiled=True)


def gathered(block, axis):
    copies = jnp.broadcast_to(block[None], (lax.axis_size(axis), *block.shape))
    return exchange(copies, axis)


def tile_major(blocks, tile_size):
    n, rows, width = blocks.shape
    per_tile = tile_size // width
    tiles = blocks.reshape(n // per_tile, per_tile, rows, width)
    return jnp.swapaxes(tiles, 1, 2).reshape(n // per_tile, rows, tile_size)


def col_summed(parts, cols):
    tiles, rows, tile_size = parts.shape
    width = tiles * tile_size // cols
    per_tile = tile_size // width
    blocks = jnp.swapaxes(parts.reshape(tiles, rows, per_tile, width), 1, 2)
    blocks = exchange(blocks.reshape(cols, rows, width), "col")
    return jnp.sum(blocks.astype(jnp.float32), axis=0).astype(jnp.bfloat16)


def per_device(tokens, upstream, w_in, in_codes, w_out, out_codes):
    tile_size = w_in.shape[3]
    cols, rows = lax.axis_size("col"), lax.axis_size("row")
    tile_rows = D // tile_size
    tile_cols = FF // (tile_size * cols)
    row = lax.axis_index("row")
    in_row, in_col, in_filled = split_codes(in_codes[0], tile_cols)
    out_row, out_col, out_filled = split_codes(out_codes[0], tile_cols)
    in_j = selector(in_col, in_filled, tile_cols).astype(jnp.float32)
    out_j = selector(out_col, out_filled, tile_cols).astype(jnp.float32)
    in_i = selector(in_row, in_filled, tile_rows).astype(jnp.float32)
    out_i = selector(out_row, out_filled, tile_rows).astype(jnp.float32)
    highest = lax.Precision.HIGHEST
    f32 = jnp.float32

    token_tiles = tile_major(gathered(tokens, "col"), tile_size)
    tiles_in = gathered(w_in[0, 0], "row")
    up_tiles = tile_major(gathered(upstream, "col"), tile_size)
    tiles_out = gathered(w_out[0, 0], "row")

    picked_tokens = jnp.take(token_tiles, in_row, axis=0)
    picked_up = jnp.take(up_tiles, out_row, axis=0)
    token_slots = exchange(picked_tokens, "row")
    upstream_slots = exchange(picked_up, "row")

    products = jnp.einsum("ktd,kdn->ktn", picked_tokens, tiles_in, preferred_element_type=f32)
    hidden = jnp.sum(products[:, None] * in_j[:, :, None, None], axis=0)
    activ = jax.nn.silu(hidden).astype(jnp.bfloat16)
    picked_activ = jnp.take(activ, out_col, axis=0)
    activ_slots = exchange(picked_activ, "row")

    products = jnp.einsum("ktf,kfd->ktd", picked_activ, tiles_out, preferred_element_type=f32)
    layer_part = jnp.einsum("ktd,ki->itd", products, out_i, precision=highest)
    layer_out = col_summed(layer_part.astype(jnp.bfloat16), cols)

    products = jnp.einsum("ktd,kfd->ktf", picked_up, tiles_out, preferred_element_type=f32)
    grad_activ = jnp.sum(products[:, None] * out_j[:, :, None, None], axis=0)
    grad_hidden = (grad_activ * silu_slope(hidden)).astype(jnp.bfloat16)
    picked_grad = jnp.take(grad_hidden, in_col, axis=0)
    grad_slots = exchange(picked_grad, "row")

    products = jnp.einsum("ktf,kdf->ktd", picked_grad, tiles_in, preferred_element_type=f32)
    input_part = jnp.einsum("ktd,ki->itd", products, in_i, precision=highest)
    grad_tokens = col_summed(input_part.astype(jnp.bfloat16), cols)

    mine_in = lax.dynamic_index_in_dim(in_filled, row, keepdims=False)
    mine_out = lax.dynamic_index_in_dim(out_filled, row, keepdims=False)
    grad_w_in = jnp.einsum("rtd,rtn->dn", token_slots, grad_slots, preferred_element_type=f32)
    grad_w_in = jnp.where(mine_in, grad_w_in, 0.0).astype(jnp.bfloat16)[None, None]
    grad_w_out = jnp.einsum("rtf,rtd->fd", activ_slots, upstream_slots, preferred_element_type=f32)
    grad_w_out = jnp.where(mine_out, grad_w_out, 0.0).astype(jnp.bfloat16)[None, None]
    return (layer_out, grad_tokens, grad_w_in, grad_w_out)


def solution(mesh):
    placed = (
        P("row", "col"),
        P("row", "col"),
        P("col", "row", None, None),
        P("col", None),
        P("col", "row", None, None),
        P("col", None),
    )
    return jax.shard_map(
        per_device,
        mesh=mesh,
        in_specs=placed,
        out_specs=(
            P("row", "col"),
            P("row", "col"),
            P("col", "row", None, None),
            P("col", "row", None, None),
        ),
        check_vma=False,
    )
```

```python
import jax
import jax.numpy as jnp
from jax import lax
from jax.experimental import pallas as pl
from jax.experimental.pallas import tpu as pltpu
from jax.sharding import PartitionSpec as P

RING = 8
BF, F32 = jnp.bfloat16, jnp.float32


class Place:
    def __init__(self):
        row, col = lax.axis_index("row"), lax.axis_index("col")
        self.row, self.col = row, col
        self.z, self.lo = row // 2, row % 2
        self.hi, self.y, self.core = col // (2 * RING), (col // 2) % RING, col % 2

    def row_at(self, dz=0, lo=None):
        return lax.rem(self.z + dz + RING, RING) * 2 + (self.lo if lo is None else lo)

    def col_at(self, dy=0, hi=None, core=None):
        y = lax.rem(self.y + dy + RING, RING)
        hi = self.hi if hi is None else hi
        return (hi * RING + y) * 2 + (self.core if core is None else core)

    def peers(self):
        return {
            "z+": (self.row_at(1), self.col),
            "z-": (self.row_at(-1), self.col),
            "lo": (self.row_at(0, 1 - self.lo), self.col),
            "y+": (self.row, self.col_at(1)),
            "y-": (self.row, self.col_at(-1)),
            "hi": (self.row, self.col_at(0, 1 - self.hi)),
            "core": (self.row, self.col_at(0, None, 1 - self.core)),
        }


def meet(peers):
    barrier = pltpu.get_barrier_semaphore()
    for device in peers.values():
        pl.semaphore_signal(barrier, inc=1, device_id=device, device_id_type=pl.DeviceIdType.MESH)
    pl.semaphore_wait(barrier, len(peers))


class Sender:
    def __init__(self, sems, peers):
        self.sems, self.peers, self.started = sems, peers, []

    def copy(self, src, dst, recv_sem, peer):
        copy = pltpu.make_async_remote_copy(
            src_ref=src,
            dst_ref=dst,
            send_sem=self.sems.at[len(self.started)],
            recv_sem=recv_sem,
            device_id=self.peers[peer],
            device_id_type=pl.DeviceIdType.MESH,
        )
        copy.start()
        self.started.append(copy)

    def arrived(self, dst, recv_sem):
        pltpu.make_async_remote_copy(
            src_ref=dst,
            dst_ref=dst,
            send_sem=self.sems.at[0],
            recv_sem=recv_sem,
            device_id=self.peers["core"],
            device_id_type=pl.DeviceIdType.MESH,
        ).wait_recv()

    def drain(self):
        for copy in self.started:
            copy.wait_send()


GATHER_SENDS = 64


def gather_kernel(x_ref, wi_ref, wo_ref, xg, wig, wog, send_sems, x_sems, wi_sems, wo_sems, own_sems):
    at = Place()
    peers = at.peers()
    meet(peers)
    out = Sender(send_sems, peers)
    own = [
        pltpu.make_async_copy(x_ref, xg.at[at.col], own_sems.at[0]),
        pltpu.make_async_copy(wi_ref, wig.at[at.row], own_sems.at[1]),
        pltpu.make_async_copy(wo_ref, wog.at[at.row], own_sems.at[2]),
    ]

    def x_send(src, col, *to):
        for peer in to:
            out.copy(src, xg.at[col], x_sems.at[col], peer)

    def wi_send(src, row, *to):
        for peer in to:
            out.copy(src, wig.at[row], wi_sems.at[row], peer)

    def wo_send(src, row, *to):
        for peer in to:
            out.copy(src, wog.at[row], wo_sems.at[row], peer)

    x_send(x_ref, at.col, "hi", "y+", "y-", "core")
    wi_send(wi_ref, at.row, "lo", "z+", "z-")
    wo_send(wo_ref, at.row, "z+", "z-", "lo")
    for copy in own:
        copy.start()

    def x_pass(col, *to):
        out.arrived(xg.at[col], x_sems.at[col])
        x_send(xg.at[col], col, *to)

    def wi_pass(row, *to):
        out.arrived(wig.at[row], wi_sems.at[row])
        wi_send(wig.at[row], row, *to)

    def wo_pass(row, *to):
        out.arrived(wog.at[row], wo_sems.at[row])
        wo_send(wog.at[row], row, *to)

    x_pass(at.col_at(0, 1 - at.hi), "y+", "y-", "core")
    wi_pass(at.row_at(0, 1 - at.lo), "z+", "z-")
    half = RING // 2
    for step in range(1, half + 1):
        for sign, mark in ((-1, "+"), (1, "-")):
            if sign == 1 and step == half:
                continue
            last = step == half if sign == -1 else step == half - 1
            for hi in (at.hi, 1 - at.hi):
                x_pass(at.col_at(sign * step, hi), *(() if last else ("y" + mark,)), "core")
        for sign, mark in ((-1, "+"), (1, "-")):
            if sign == 1 and step == half:
                continue
            last = step == half if sign == -1 else step == half - 1
            onward = () if last else ("z" + mark,)
            wi_pass(at.row_at(sign * step), *onward)
            wo_pass(at.row_at(sign * step), *onward, "lo")
            wi_pass(at.row_at(sign * step, 1 - at.lo), *onward)
    for step in range(RING):
        for hi in range(2):
            col = at.col_at(step, hi, 1 - at.core)
            out.arrived(xg.at[col], x_sems.at[col])
        row = at.row_at(step, 1 - at.lo)
        out.arrived(wog.at[row], wo_sems.at[row])
    out.drain()
    for copy in own:
        copy.wait()


def gather(x, wi, wo):
    any_space = pl.BlockSpec(memory_space=pl.ANY)
    tile = wi.shape
    return pl.pallas_call(
        gather_kernel,
        name="gather_all",
        out_shape=(
            jax.ShapeDtypeStruct((4 * RING, *x.shape), BF),
            jax.ShapeDtypeStruct((2 * RING, *tile), BF),
            jax.ShapeDtypeStruct((2 * RING, *tile), BF),
        ),
        in_specs=[any_space] * 3,
        out_specs=(any_space,) * 3,
        scratch_shapes=[
            pltpu.SemaphoreType.DMA((GATHER_SENDS,)),
            pltpu.SemaphoreType.DMA((4 * RING,)),
            pltpu.SemaphoreType.DMA((2 * RING,)),
            pltpu.SemaphoreType.DMA((2 * RING,)),
            pltpu.SemaphoreType.DMA((3,)),
        ],
        compiler_params=pltpu.CompilerParams(collective_id=0, has_side_effects=True),
    )(x, wi, wo)


def dot(a, b, contract):
    return lax.dot_general(a, b, (contract, ((), ())), preferred_element_type=F32)


def panel_kernel(in_codes, out_codes, x, wi, wo, parts, grads, hid, gact, act, gh, lay, inp):
    slots = wi.shape[0]
    hid[...] = jnp.zeros_like(hid)
    gact[...] = jnp.zeros_like(gact)
    lay[...] = jnp.zeros_like(lay)
    inp[...] = jnp.zeros_like(inp)

    def codes(ref, k):
        code = ref[k]
        clipped = jnp.maximum(code, 0)
        return clipped // 2, clipped % 2, code >= 0

    def tile(which, i):
        return jnp.concatenate([x[2 * i, which], x[2 * i + 1, which]], axis=1)

    def inward(k, _):
        i, j, filled = codes(in_codes, k)

        @pl.when(filled)
        def _():
            hid[j] += dot(tile(0, i), wi[k], ((1,), (0,)))

        i2, j2, filled2 = codes(out_codes, k)

        @pl.when(filled2)
        def _():
            gact[j2] += dot(tile(1, i2), wo[k], ((1,), (1,)))

        return 0

    lax.fori_loop(0, slots, inward, 0)
    for j in range(2):
        h = hid[j]
        s = jax.nn.sigmoid(h)
        act[j] = (h * s).astype(BF)
        gh[j] = (gact[j] * (s * (1.0 + h * (1.0 - s)))).astype(BF)

    def outward(k, _):
        i, j, filled = codes(in_codes, k)

        @pl.when(filled)
        def _():
            g = gh[j]
            inp[i] += dot(g, wi[k], ((1,), (1,)))
            grads[0, k] = dot(tile(0, i), g, ((0,), (0,))).astype(BF)

        @pl.when(jnp.logical_not(filled))
        def _():
            grads[0, k] = jnp.zeros(grads.shape[2:], BF)

        i2, j2, filled2 = codes(out_codes, k)

        @pl.when(filled2)
        def _():
            a = act[j2]
            lay[i2] += dot(a, wo[k], ((1,), (0,)))
            grads[1, k] = dot(a, tile(1, i2), ((0,), (0,))).astype(BF)

        @pl.when(jnp.logical_not(filled2))
        def _():
            grads[1, k] = jnp.zeros(grads.shape[2:], BF)

        return 0

    lax.fori_loop(0, slots, outward, 0)

    def round_up(i, _):
        for t, total in enumerate((lay, inp)):
            full = total[i].astype(BF)
            for core in range(2):
                parts[core, i, t] = full[:, core * 128 : (core + 1) * 128]
        return 0

    lax.fori_loop(0, lay.shape[0], round_up, 0)


def panel(in_codes, out_codes, x, wi, wo):
    cols, _, rows, width = x.shape
    tiles = cols // 2
    slots, size, _ = wi.shape
    vmem, smem = pl.BlockSpec(memory_space=pltpu.VMEM), pl.BlockSpec(memory_space=pltpu.SMEM)
    return pl.pallas_call(
        panel_kernel,
        name="panel",
        out_shape=(
            jax.ShapeDtypeStruct((2, tiles, 2, rows, width), BF),
            jax.ShapeDtypeStruct((2, slots, size, size), BF),
        ),
        in_specs=[smem, smem, vmem, vmem, vmem],
        out_specs=(vmem, vmem),
        scratch_shapes=[
            pltpu.VMEM((2, rows, size), F32),
            pltpu.VMEM((2, rows, size), F32),
            pltpu.VMEM((2, rows, size), BF),
            pltpu.VMEM((2, rows, size), BF),
            pltpu.VMEM((tiles, rows, size), F32),
            pltpu.VMEM((tiles, rows, size), F32),
        ],
        compiler_params=pltpu.CompilerParams(vmem_limit_bytes=48 << 20),
    )(in_codes, out_codes, x, wi, wo)


REDUCE_SENDS = 48


def reduce_kernel(
    parts, grads, red, grad_out,
    pair_buf, chip_sum, y_buf, z_buf, hi_buf, lo_buf, hi_sum, lo_sum,
    send_sems, pair_sem, y_sems, z_sems, hi_sem, lo_sem,
):
    at = Place()
    peers = at.peers()
    meet(peers)
    out = Sender(send_sems, peers)
    half = RING // 2
    far = (half, half - 1)
    marks = ("+", "-")
    signs = (1, -1)

    def wide(value):
        return value.astype(F32)

    def z_of(sign, dist):
        return lax.rem(at.z + sign * dist + RING, RING)

    def y_of(sign, dist):
        return lax.rem(at.y + sign * dist + RING, RING)

    out.copy(parts.at[1 - at.core], pair_buf, pair_sem, "core")
    for d in range(2):
        for lo in range(2):
            for t in range(2):
                slot = d * half
                out.copy(
                    grads.at[t, z_of(signs[d], far[d]) * 2 + lo],
                    z_buf.at[slot, lo, t],
                    z_sems.at[slot, lo, t],
                    "z" + marks[d],
                )
    out.arrived(pair_buf, pair_sem)
    for hi in range(2):
        for y in range(RING):
            i = hi * RING + y
            chip_sum[y, hi] = (wide(parts[at.core, i]) + wide(pair_buf[i])).astype(BF)
    for d in range(2):
        slot = d * half
        out.copy(chip_sum.at[y_of(signs[d], far[d])], y_buf.at[slot], y_sems.at[slot], "y" + marks[d])

    for step in range(1, half):
        for d in range(2):
            if step >= far[d]:
                continue
            slot = d * half + step - 1
            out.arrived(y_buf.at[slot], y_sems.at[slot])
            target = y_of(signs[d], far[d] - step)
            y_buf[slot] = (wide(y_buf[slot]) + wide(chip_sum[target])).astype(BF)
            out.copy(y_buf.at[slot], y_buf.at[slot + 1], y_sems.at[slot + 1], "y" + marks[d])
        for lo in range(2):
            for t in range(2):
                for d in range(2):
                    if step >= far[d]:
                        continue
                    slot = d * half + step - 1
                    out.arrived(z_buf.at[slot, lo, t], z_sems.at[slot, lo, t])
                    target = z_of(signs[d], far[d] - step) * 2 + lo
                    z_buf[slot, lo, t] = (wide(z_buf[slot, lo, t]) + wide(grads[t, target])).astype(BF)
                    out.copy(
                        z_buf.at[slot, lo, t],
                        z_buf.at[slot + 1, lo, t],
                        z_sems.at[slot + 1, lo, t],
                        "z" + marks[d],
                    )

    ends = [d * half + far[d] - 1 for d in range(2)]
    for slot in ends:
        out.arrived(y_buf.at[slot], y_sems.at[slot])

    def y_total(hi):
        return wide(chip_sum[at.y, hi]) + wide(y_buf[ends[0], hi]) + wide(y_buf[ends[1], hi])

    hi_sum[...] = y_total(1 - at.hi).astype(BF)
    out.copy(hi_sum, hi_buf, hi_sem, "hi")

    def z_total(lo, t):
        return wide(grads[t, at.z * 2 + lo]) + wide(z_buf[ends[0], lo, t]) + wide(z_buf[ends[1], lo, t])

    for t in range(2):
        for lo in range(2):
            for slot in ends:
                out.arrived(z_buf.at[slot, lo, t], z_sems.at[slot, lo, t])
        lo_sum[t] = z_total(1 - at.lo, t).astype(BF)
        out.copy(lo_sum.at[t], lo_buf.at[t], lo_sem.at[t], "lo")
    out.arrived(hi_buf, hi_sem)
    red[...] = (y_total(at.hi) + wide(hi_buf[...])).astype(BF)
    for t in range(2):
        out.arrived(lo_buf.at[t], lo_sem.at[t])
        grad_out[t] = (z_total(at.lo, t) + wide(lo_buf[t])).astype(BF)
    out.drain()


def reduce(parts, grads):
    _, tiles, two, rows, width = parts.shape
    size = grads.shape[-1]
    vmem = pl.BlockSpec(memory_space=pltpu.VMEM)
    block, tile = (two, rows, width), (size, size)
    return pl.pallas_call(
        reduce_kernel,
        name="reduce_all",
        out_shape=(jax.ShapeDtypeStruct(block, BF), jax.ShapeDtypeStruct((2, *tile), BF)),
        in_specs=[vmem, vmem],
        out_specs=(vmem, vmem),
        scratch_shapes=[
            pltpu.VMEM((tiles, *block), BF),
            pltpu.VMEM((RING, 2, *block), BF),
            pltpu.VMEM((RING - 1, 2, *block), BF),
            pltpu.VMEM((RING - 1, 2, 2, *tile), BF),
            pltpu.VMEM(block, BF),
            pltpu.VMEM((2, *tile), BF),
            pltpu.VMEM(block, BF),
            pltpu.VMEM((2, *tile), BF),
            pltpu.SemaphoreType.DMA((REDUCE_SENDS,)),
            pltpu.SemaphoreType.DMA,
            pltpu.SemaphoreType.DMA((RING - 1,)),
            pltpu.SemaphoreType.DMA((RING - 1, 2, 2)),
            pltpu.SemaphoreType.DMA,
            pltpu.SemaphoreType.DMA((2,)),
        ],
        compiler_params=pltpu.CompilerParams(
            collective_id=1, has_side_effects=True, vmem_limit_bytes=48 << 20
        ),
    )(parts, grads)


def per_device(tokens, upstream, w_in, in_codes, w_out, out_codes):
    x, wi, wo = gather(jnp.stack([tokens, upstream]), w_in[0, 0], w_out[0, 0])
    parts, grads = panel(in_codes[0], out_codes[0], x, wi, wo)
    red, grad = reduce(parts, grads)
    return red[0], red[1], grad[0][None, None], grad[1][None, None]


def solution(mesh):
    placed = (
        P("row", "col"),
        P("row", "col"),
        P("col", "row", None, None),
        P("col", None),
        P("col", "row", None, None),
        P("col", None),
    )
    return jax.shard_map(
        per_device,
        mesh=mesh,
        in_specs=placed,
        out_specs=(
            P("row", "col"),
            P("row", "col"),
            P("col", "row", None, None),
            P("col", "row", None, None),
        ),
        check_vma=False,
    )
```

```python
import jax
import jax.numpy as jnp
from jax import lax
from jax.experimental import pallas as pl
from jax.experimental.pallas import tpu as pltpu
from jax.sharding import PartitionSpec as P

RING = 8
BF, F32 = jnp.bfloat16, jnp.float32


class Place:
    def __init__(self):
        row, col = lax.axis_index("row"), lax.axis_index("col")
        self.row, self.col = row, col
        self.z, self.lo = row // 2, row % 2
        self.hi, self.y, self.core = col // (2 * RING), (col // 2) % RING, col % 2

    def row_at(self, dz=0, lo=None):
        return lax.rem(self.z + dz + RING, RING) * 2 + (self.lo if lo is None else lo)

    def col_at(self, dy=0, hi=None, core=None):
        y = lax.rem(self.y + dy + RING, RING)
        hi = self.hi if hi is None else hi
        return (hi * RING + y) * 2 + (self.core if core is None else core)

    def peers(self):
        return {
            "z+": (self.row_at(1), self.col),
            "z-": (self.row_at(-1), self.col),
            "lo": (self.row_at(0, 1 - self.lo), self.col),
            "y+": (self.row, self.col_at(1)),
            "y-": (self.row, self.col_at(-1)),
            "hi": (self.row, self.col_at(0, 1 - self.hi)),
            "core": (self.row, self.col_at(0, None, 1 - self.core)),
        }


def meet(peers):
    barrier = pltpu.get_barrier_semaphore()
    for device in peers.values():
        pl.semaphore_signal(barrier, inc=1, device_id=device, device_id_type=pl.DeviceIdType.MESH)
    pl.semaphore_wait(barrier, len(peers))


class Sender:
    def __init__(self, sems, peers):
        self.sems, self.peers, self.started = sems, peers, []

    def copy(self, src, dst, recv_sem, peer):
        copy = pltpu.make_async_remote_copy(
            src_ref=src,
            dst_ref=dst,
            send_sem=self.sems.at[len(self.started)],
            recv_sem=recv_sem,
            device_id=self.peers[peer],
            device_id_type=pl.DeviceIdType.MESH,
        )
        copy.start()
        self.started.append(copy)

    def arrived(self, dst, recv_sem):
        pltpu.make_async_remote_copy(
            src_ref=dst,
            dst_ref=dst,
            send_sem=self.sems.at[0],
            recv_sem=recv_sem,
            device_id=self.peers["core"],
            device_id_type=pl.DeviceIdType.MESH,
        ).wait_recv()

    def drain(self):
        for copy in self.started:
            copy.wait_send()


GATHER_SENDS = 96


def dot(a, b, contract):
    return lax.dot_general(a, b, (contract, ((), ())), preferred_element_type=F32)


def split_code(ref, k):
    code = ref[k]
    clipped = jnp.maximum(code, 0)
    return clipped // 2, clipped % 2, code >= 0


def token_tile(x, which, i):
    halves = [jnp.concatenate([x[lo, 2 * i, which], x[lo, 2 * i + 1, which]], axis=1) for lo in range(2)]
    return jnp.concatenate(halves, axis=0)


def gather_kernel(
    in_codes, out_codes, tokens, upstream, wi_ref, wo_ref, xg, wig, wog, act, gh,
    hid, gact, mine, theirs, send_sems, x_sems, w_sems, own_sems, swap_sems,
):
    at = Place()
    peers = at.peers()
    x_own = xg.at[at.lo, at.col]
    own = [
        pltpu.make_async_copy(tokens, x_own.at[0], own_sems.at[0]),
        pltpu.make_async_copy(upstream, x_own.at[1], own_sems.at[1]),
        pltpu.make_async_copy(wi_ref, wig.at[at.z], own_sems.at[2]),
        pltpu.make_async_copy(wo_ref, wog.at[at.z], own_sems.at[3]),
    ]
    for copy in own:
        copy.start()
    meet(peers)
    out = Sender(send_sems, peers)
    for copy in own:
        copy.wait()
    held = (wig, wog)

    def x_send(lo, col, *to):
        for peer in to:
            out.copy(xg.at[lo, col], xg.at[lo, col], x_sems.at[lo, col], peer)

    def x_pass(lo, col, *to):
        out.arrived(xg.at[lo, col], x_sems.at[lo, col])
        x_send(lo, col, *to)

    def w_send(t, z, *to):
        for peer in to:
            out.copy(held[t].at[z], held[t].at[z], w_sems.at[t, z], peer)

    def w_pass(t, z, *to):
        out.arrived(held[t].at[z], w_sems.at[t, z])
        w_send(t, z, *to)

    x_send(at.lo, at.col, "lo", "hi", "y+", "y-")
    for t in range(2):
        w_send(t, at.z, "z+", "z-")
    x_send(at.lo, at.col, "core")
    x_pass(1 - at.lo, at.col, "hi", "y+", "y-", "core")
    x_pass(at.lo, at.col_at(0, 1 - at.hi), "y+", "y-", "core")
    x_pass(1 - at.lo, at.col_at(0, 1 - at.hi), "y+", "y-", "core")
    half = RING // 2
    flows = ((-1, "+"), (1, "-"))
    for step in range(1, half + 1):
        for d, (sign, mark) in enumerate(flows):
            for n, (lo, hi) in enumerate(((at.lo, at.hi), (1 - at.lo, at.hi), (at.lo, 1 - at.hi), (1 - at.lo, 1 - at.hi))):
                if step == half and n % 2 != d:
                    continue
                onward = step < half - 1 or (step == half - 1 and n % 2 == d)
                x_pass(lo, at.col_at(sign * step, hi), *(("y" + mark,) if onward else ()), "core")
        for t in range(2):
            for d, (sign, mark) in enumerate(flows):
                if step == half and t != d:
                    continue
                onward = step < half - 1 or (step == half - 1 and t == d)
                w_pass(t, lax.rem(at.z + sign * step + RING, RING), *(("z" + mark,) if onward else ()))
    for step in range(RING):
        for hi in range(2):
            for lo in range(2):
                col = at.col_at(step, hi, 1 - at.core)
                out.arrived(xg.at[lo, col], x_sems.at[lo, col])

    hid[...] = jnp.zeros_like(hid)
    gact[...] = jnp.zeros_like(gact)

    def inward(codes, which, weights, total, contract):
        def one(k, _):
            i, j, filled = split_code(codes, k)
            product = dot(token_tile(xg, which, i), weights[k], contract)
            for col in range(2):
                total[col] += jnp.where(jnp.logical_and(filled, j == col), product, 0.0)
            return 0

        lax.fori_loop(0, RING, one, 0)
        mine[which] = total[...].astype(BF)
        out.copy(mine.at[which], theirs.at[which], swap_sems.at[which], "lo")

    inward(in_codes, 0, wig, hid, ((1,), (0,)))
    inward(out_codes, 1, wog, gact, ((1,), (1,)))
    out.arrived(theirs.at[0], swap_sems.at[0])
    out.arrived(theirs.at[1], swap_sems.at[1])
    for j in range(2):
        h = hid[j] + theirs[0, j].astype(F32)
        s = jax.nn.sigmoid(h)
        act[j] = (h * s).astype(BF)
        gh[j] = ((gact[j] + theirs[1, j].astype(F32)) * (s * (1.0 + h * (1.0 - s)))).astype(BF)
    out.drain()


def specs():
    return pl.BlockSpec(memory_space=pltpu.VMEM), pl.BlockSpec(memory_space=pltpu.SMEM)


def gather(in_codes, out_codes, tokens, upstream, wi, wo):
    vmem, smem = specs()
    size = wi.shape[0]
    pair = (2, 2 * tokens.shape[0], size)
    return pl.pallas_call(
        gather_kernel,
        name="gather_all",
        out_shape=(
            jax.ShapeDtypeStruct((2, 4 * RING, 2, *tokens.shape), BF),
            jax.ShapeDtypeStruct((RING, *wi.shape), BF),
            jax.ShapeDtypeStruct((RING, *wi.shape), BF),
            jax.ShapeDtypeStruct(pair, BF),
            jax.ShapeDtypeStruct(pair, BF),
        ),
        in_specs=[smem, smem, vmem, vmem, vmem, vmem],
        out_specs=(vmem,) * 5,
        scratch_shapes=[
            pltpu.VMEM(pair, F32),
            pltpu.VMEM(pair, F32),
            pltpu.VMEM((2, *pair), BF),
            pltpu.VMEM((2, *pair), BF),
            pltpu.SemaphoreType.DMA((GATHER_SENDS,)),
            pltpu.SemaphoreType.DMA((2, 4 * RING)),
            pltpu.SemaphoreType.DMA((2, RING)),
            pltpu.SemaphoreType.DMA((4,)),
            pltpu.SemaphoreType.DMA((2,)),
        ],
        compiler_params=pltpu.CompilerParams(
            collective_id=0, has_side_effects=True, vmem_limit_bytes=32 << 20
        ),
    )(in_codes, out_codes, tokens, upstream, wi, wo)


def panel_kernel(in_codes, out_codes, act, gh, wi, wo, parts, lay, inp):
    lay[...] = jnp.zeros_like(lay)
    inp[...] = jnp.zeros_like(inp)

    def outward(k, _):
        i, j, filled = split_code(in_codes, k)

        @pl.when(filled)
        def _():
            inp[i] += dot(gh[j], wi[k], ((1,), (1,)))

        i2, j2, filled2 = split_code(out_codes, k)

        @pl.when(filled2)
        def _():
            lay[i2] += dot(act[j2], wo[k], ((1,), (0,)))

        return 0

    lax.fori_loop(0, wi.shape[0], outward, 0)
    rows, width = parts.shape[-2:]

    def round_up(i, _):
        for t, total in enumerate((lay, inp)):
            full = total[i].astype(BF)
            for core in range(2):
                for lo in range(2):
                    parts[core, i % RING, lo, i // RING, t] = full[
                        lo * rows : (lo + 1) * rows, core * width : (core + 1) * width
                    ]
        return 0

    lax.fori_loop(0, lay.shape[0], round_up, 0)


def panel(in_codes, out_codes, act, gh, wi, wo, rows):
    vmem, smem = specs()
    size = wi.shape[-1]
    total = pltpu.VMEM((2 * RING, 2 * rows, size), F32)
    return pl.pallas_call(
        panel_kernel,
        name="panel",
        out_shape=jax.ShapeDtypeStruct((2, RING, 2, 2, 2, rows, size // 2), BF),
        in_specs=[smem, smem, vmem, vmem, vmem, vmem],
        out_specs=vmem,
        scratch_shapes=[total, total],
        compiler_params=pltpu.CompilerParams(vmem_limit_bytes=32 << 20),
    )(in_codes, out_codes, act, gh, wi, wo)


REDUCE_SENDS = 48


def reduce_kernel(
    in_codes, out_codes, x, act, gh, parts, layer, grad_tokens, grad_in, grad_out,
    pair_buf, y_far, y_buf, z_far, z_buf, hi_sum, hi_buf, lo_sum, lo_buf,
    send_sems, pair_sems, y_sems, z_sems, end_sems,
):
    at = Place()
    peers = at.peers()
    meet(peers)
    out = Sender(send_sems, peers)
    half = RING // 2
    marks, signs = ("+", "-"), (1, -1)

    def wide(value):
        return value.astype(F32)

    def y_of(dist):
        return lax.rem(at.y + dist + RING, RING)

    def z_of(dist):
        return lax.rem(at.z + dist + RING, RING)

    def share(t, k):
        if t == 0:
            i, j, filled = split_code(in_codes, k)
            product = dot(token_tile(x, 0, i), gh[j], ((0,), (0,)))
        else:
            i, j, filled = split_code(out_codes, k)
            product = dot(act[j], token_tile(x, 1, i), ((0,), (0,)))
        return jnp.where(filled, product, 0.0)

    def chip(y, lo):
        return wide(parts[at.core, y, lo]) + wide(pair_buf[y, lo])

    order = [half] + [sign * dist for dist in range(half - 1, 0, -1) for sign in signs] + [0]
    for dist in order:
        y = y_of(dist)
        out.copy(parts.at[1 - at.core, y], pair_buf.at[y], pair_sems.at[y], "core")
    for d in range(2):
        z_far[d] = share(d, z_of(half)).astype(BF)
        out.copy(z_far.at[d], z_buf.at[d, 0, d], z_sems.at[d, 0, d], "z" + marks[d])
    y = y_of(half)
    out.arrived(pair_buf.at[y], pair_sems.at[y])
    for d in range(2):
        y_far[d] = chip(y, d).astype(BF)
        out.copy(y_far.at[d], y_buf.at[d, 0, d], y_sems.at[d, 0, d], "y" + marks[d])

    for step in range(1, half):
        for d in range(2):
            y = y_of(signs[d] * (half - step))
            out.arrived(pair_buf.at[y], pair_sems.at[y])
            for lo in (d, 1 - d):
                value = chip(y, lo)
                slot = y_buf.at[d, step - 1, lo]
                if step > 1 or lo == d:
                    out.arrived(slot, y_sems.at[d, step - 1, lo])
                    value = value + wide(slot[...])
                slot[...] = value.astype(BF)
                out.copy(slot, y_buf.at[d, step, lo], y_sems.at[d, step, lo], "y" + marks[d])
        for d in range(2):
            k = z_of(signs[d] * (half - step))
            for t in (d, 1 - d):
                value = share(t, k)
                slot = z_buf.at[d, step - 1, t]
                if step > 1 or t == d:
                    out.arrived(slot, z_sems.at[d, step - 1, t])
                    value = value + wide(slot[...])
                slot[...] = value.astype(BF)
                out.copy(slot, z_buf.at[d, step, t], z_sems.at[d, step, t], "z" + marks[d])

    out.arrived(pair_buf.at[at.y], pair_sems.at[at.y])
    for lo in range(2):
        for d in range(2):
            out.arrived(y_buf.at[d, half - 1, lo], y_sems.at[d, half - 1, lo])

    def y_total(lo, hi):
        value = wide(parts[at.core, at.y, lo, hi]) + wide(pair_buf[at.y, lo, hi])
        return value + wide(y_buf[0, half - 1, lo, hi]) + wide(y_buf[1, half - 1, lo, hi])

    for lo in range(2):
        hi_sum[lo] = y_total(lo, 1 - at.hi).astype(BF)
    out.copy(hi_sum, hi_buf, end_sems.at[0], "hi")
    own = [share(t, at.z) for t in range(2)]
    out.arrived(hi_buf, end_sems.at[0])
    lo_sum[...] = (y_total(1 - at.lo, at.hi) + wide(hi_buf[1 - at.lo])).astype(BF)
    out.copy(lo_sum, lo_buf, end_sems.at[1], "lo")
    for t, result in enumerate((grad_in, grad_out)):
        value = own[t]
        for d in range(2):
            slot = z_buf.at[d, half - 1, t]
            out.arrived(slot, z_sems.at[d, half - 1, t])
            value = value + wide(slot[...])
        result[...] = value.astype(BF)
    out.arrived(lo_buf, end_sems.at[1])
    total = y_total(at.lo, at.hi) + wide(hi_buf[at.lo]) + wide(lo_buf[...])
    layer[...] = total[0].astype(BF)
    grad_tokens[...] = total[1].astype(BF)
    out.drain()


def reduce(in_codes, out_codes, x, act, gh, parts):
    vmem, smem = specs()
    rows, width = parts.shape[-2:]
    size = act.shape[-1]
    half = RING // 2
    block, tile = (2, rows, width), (size, size)
    return pl.pallas_call(
        reduce_kernel,
        name="reduce_all",
        out_shape=(
            jax.ShapeDtypeStruct((rows, width), BF),
            jax.ShapeDtypeStruct((rows, width), BF),
            jax.ShapeDtypeStruct(tile, BF),
            jax.ShapeDtypeStruct(tile, BF),
        ),
        in_specs=[smem, smem, vmem, vmem, vmem, vmem],
        out_specs=(vmem,) * 4,
        scratch_shapes=[
            pltpu.VMEM((RING, 2, 2, *block), BF),
            pltpu.VMEM((2, 2, *block), BF),
            pltpu.VMEM((2, half, 2, 2, *block), BF),
            pltpu.VMEM((2, *tile), BF),
            pltpu.VMEM((2, half, 2, *tile), BF),
            pltpu.VMEM((2, *block), BF),
            pltpu.VMEM((2, *block), BF),
            pltpu.VMEM(block, BF),
            pltpu.VMEM(block, BF),
            pltpu.SemaphoreType.DMA((REDUCE_SENDS,)),
            pltpu.SemaphoreType.DMA((RING,)),
            pltpu.SemaphoreType.DMA((2, half, 2)),
            pltpu.SemaphoreType.DMA((2, half, 2)),
            pltpu.SemaphoreType.DMA((2,)),
        ],
        compiler_params=pltpu.CompilerParams(
            collective_id=1, has_side_effects=True, vmem_limit_bytes=32 << 20
        ),
    )(in_codes, out_codes, x, act, gh, parts)


def per_device(tokens, upstream, w_in, in_codes, w_out, out_codes):
    lo = lax.axis_index("row") % 2
    in_codes, out_codes = (
        lax.dynamic_index_in_dim(codes.reshape(RING, 2), lo, axis=1, keepdims=False)
        for codes in (in_codes, out_codes)
    )
    x, wi, wo, act, gh = gather(in_codes, out_codes, tokens, upstream, w_in[0, 0], w_out[0, 0])
    parts = panel(in_codes, out_codes, act, gh, wi, wo, tokens.shape[0])
    layer, grad_tokens, grad_in, grad_out = reduce(in_codes, out_codes, x, act, gh, parts)
    return layer, grad_tokens, grad_in[None, None], grad_out[None, None]


def solution(mesh):
    placed = (
        P("row", "col"),
        P("row", "col"),
        P("col", "row", None, None),
        P("col", None),
        P("col", "row", None, None),
        P("col", None),
    )
    return jax.shard_map(
        per_device,
        mesh=mesh,
        in_specs=placed,
        out_specs=(
            P("row", "col"),
            P("row", "col"),
            P("col", "row", None, None),
            P("col", "row", None, None),
        ),
        check_vma=False,
    )
```

```python
import jax
import jax.numpy as jnp
from jax import lax
from jax.experimental import pallas as pl
from jax.experimental.pallas import tpu as pltpu
from jax.sharding import PartitionSpec as P

RING = 8
BF, F32 = jnp.bfloat16, jnp.float32


class Place:
    def __init__(self):
        row, col = lax.axis_index("row"), lax.axis_index("col")
        self.row, self.col = row, col
        self.z, self.lo = row // 2, row % 2
        self.hi, self.y, self.core = col // (2 * RING), (col // 2) % RING, col % 2

    def row_at(self, dz=0, lo=None):
        return lax.rem(self.z + dz + RING, RING) * 2 + (self.lo if lo is None else lo)

    def col_at(self, dy=0, hi=None, core=None):
        y = lax.rem(self.y + dy + RING, RING)
        hi = self.hi if hi is None else hi
        return (hi * RING + y) * 2 + (self.core if core is None else core)

    def peers(self):
        return {
            "z+": (self.row_at(1), self.col),
            "z-": (self.row_at(-1), self.col),
            "lo": (self.row_at(0, 1 - self.lo), self.col),
            "y+": (self.row, self.col_at(1)),
            "y-": (self.row, self.col_at(-1)),
            "hi": (self.row, self.col_at(0, 1 - self.hi)),
            "diag": (self.row_at(0, 1 - self.lo), self.col_at(0, 1 - self.hi)),
            "core": (self.row, self.col_at(0, None, 1 - self.core)),
        }


def meet(peers):
    barrier = pltpu.get_barrier_semaphore()
    for device in peers.values():
        pl.semaphore_signal(barrier, inc=1, device_id=device, device_id_type=pl.DeviceIdType.MESH)
    pl.semaphore_wait(barrier, len(peers))


class Sender:
    def __init__(self, sems, peers):
        self.sems, self.peers, self.started = sems, peers, []

    def copy(self, src, dst, recv_sem, peer):
        copy = pltpu.make_async_remote_copy(
            src_ref=src,
            dst_ref=dst,
            send_sem=self.sems.at[len(self.started)],
            recv_sem=recv_sem,
            device_id=self.peers[peer],
            device_id_type=pl.DeviceIdType.MESH,
        )
        copy.start()
        self.started.append(copy)

    def arrived(self, dst, recv_sem):
        pltpu.make_async_remote_copy(
            src_ref=dst,
            dst_ref=dst,
            send_sem=self.sems.at[0],
            recv_sem=recv_sem,
            device_id=self.peers["core"],
            device_id_type=pl.DeviceIdType.MESH,
        ).wait_recv()

    def drain(self):
        for copy in self.started:
            copy.wait_send()


GATHER_SENDS = 96


def dot(a, b, contract):
    return lax.dot_general(a, b, (contract, ((), ())), preferred_element_type=F32)


def split_code(ref, k):
    code = ref[2 * k + lax.axis_index("row") % 2]
    clipped = jnp.maximum(code, 0)
    return clipped // 2, clipped % 2, code >= 0


def token_tile(x, which, i):
    halves = [jnp.concatenate([x[lo, 2 * i, which], x[lo, 2 * i + 1, which]], axis=1) for lo in range(2)]
    return jnp.concatenate(halves, axis=0)


def gather_kernel(
    in_codes, out_codes, tokens, upstream, wi_ref, wo_ref, xg, wig, wog, act, gh,
    hid, gact, mine, theirs, send_sems, x_sems, w_sems, own_sems, swap_sems,
):
    at = Place()
    peers = at.peers()
    x_own = xg.at[at.lo, at.col]
    own = [
        pltpu.make_async_copy(tokens, x_own.at[0], own_sems.at[0]),
        pltpu.make_async_copy(upstream, x_own.at[1], own_sems.at[1]),
        pltpu.make_async_copy(wi_ref, wig.at[at.z], own_sems.at[2]),
        pltpu.make_async_copy(wo_ref, wog.at[at.z], own_sems.at[3]),
    ]
    for copy in own:
        copy.start()
    meet(peers)
    out = Sender(send_sems, peers)
    for copy in own:
        copy.wait()
    held = (wig, wog)

    def x_send(lo, col, *to):
        for peer in to:
            out.copy(xg.at[lo, col], xg.at[lo, col], x_sems.at[lo, col], peer)

    def x_pass(lo, col, *to):
        out.arrived(xg.at[lo, col], x_sems.at[lo, col])
        x_send(lo, col, *to)

    def w_send(t, z, *to):
        for peer in to:
            out.copy(held[t].at[z], held[t].at[z], w_sems.at[t, z], peer)

    def w_pass(t, z, *to):
        out.arrived(held[t].at[z], w_sems.at[t, z])
        w_send(t, z, *to)

    x_send(at.lo, at.col, "y+", "y-", "lo", "diag", "hi")
    for t in range(2):
        w_send(t, at.z, "z+", "z-")
    x_send(at.lo, at.col, "core")
    x_pass(1 - at.lo, at.col, "y+", "y-", "core")
    x_pass(at.lo, at.col_at(0, 1 - at.hi), "y+", "y-", "core")
    x_pass(1 - at.lo, at.col_at(0, 1 - at.hi), "y+", "y-", "core")
    half = RING // 2
    flows = ((-1, "+"), (1, "-"))
    kinds = ((at.lo, at.hi), (1 - at.lo, at.hi), (at.lo, 1 - at.hi), (1 - at.lo, 1 - at.hi))
    for step in range(1, half + 1):
        for n, (lo, hi) in enumerate(kinds):
            for d, (sign, mark) in enumerate(flows):
                if step == half and n % 2 != d:
                    continue
                onward = step < half - 1 or (step == half - 1 and n % 2 == d)
                x_pass(lo, at.col_at(sign * step, hi), *(("y" + mark,) if onward else ()), "core")
            if n % 2 == 1:
                continue
            t = n // 2
            for d, (sign, mark) in enumerate(flows):
                if step == half and t != d:
                    continue
                onward = step < half - 1 or (step == half - 1 and t == d)
                w_pass(t, lax.rem(at.z + sign * step + RING, RING), *(("z" + mark,) if onward else ()))
    for step in range(RING):
        for hi in range(2):
            for lo in range(2):
                col = at.col_at(step, hi, 1 - at.core)
                out.arrived(xg.at[lo, col], x_sems.at[lo, col])

    hid[...] = jnp.zeros_like(hid)
    gact[...] = jnp.zeros_like(gact)

    def inward(codes, which, weights, total, contract):
        def one(k, _):
            i, j, filled = split_code(codes, k)
            product = dot(token_tile(xg, which, i), weights[k], contract)
            for col in range(2):
                total[col] += jnp.where(jnp.logical_and(filled, j == col), product, 0.0)
            return 0

        lax.fori_loop(0, RING, one, 0)
        mine[which] = total[...].astype(BF)
        out.copy(mine.at[which], theirs.at[which], swap_sems.at[which], "lo")

    inward(in_codes, 0, wig, hid, ((1,), (0,)))
    inward(out_codes, 1, wog, gact, ((1,), (1,)))
    out.arrived(theirs.at[0], swap_sems.at[0])
    out.arrived(theirs.at[1], swap_sems.at[1])
    for j in range(2):
        h = hid[j] + theirs[0, j].astype(F32)
        s = jax.nn.sigmoid(h)
        act[j] = (h * s).astype(BF)
        gh[j] = ((gact[j] + theirs[1, j].astype(F32)) * (s * (1.0 + h * (1.0 - s)))).astype(BF)
    out.drain()


def specs():
    return pl.BlockSpec(memory_space=pltpu.VMEM), pl.BlockSpec(memory_space=pltpu.SMEM)


def gather(in_codes, out_codes, tokens, upstream, wi, wo):
    vmem, smem = specs()
    size = wi.shape[0]
    pair = (2, 2 * tokens.shape[0], size)
    return pl.pallas_call(
        gather_kernel,
        name="gather_all",
        out_shape=(
            jax.ShapeDtypeStruct((2, 4 * RING, 2, *tokens.shape), BF),
            jax.ShapeDtypeStruct((RING, *wi.shape), BF),
            jax.ShapeDtypeStruct((RING, *wi.shape), BF),
            jax.ShapeDtypeStruct(pair, BF),
            jax.ShapeDtypeStruct(pair, BF),
        ),
        in_specs=[smem, smem] + [pl.BlockSpec(memory_space=pltpu.HBM)] * 4,
        out_specs=(vmem,) * 5,
        scratch_shapes=[
            pltpu.VMEM(pair, F32),
            pltpu.VMEM(pair, F32),
            pltpu.VMEM((2, *pair), BF),
            pltpu.VMEM((2, *pair), BF),
            pltpu.SemaphoreType.DMA((GATHER_SENDS,)),
            pltpu.SemaphoreType.DMA((2, 4 * RING)),
            pltpu.SemaphoreType.DMA((2, RING)),
            pltpu.SemaphoreType.DMA((4,)),
            pltpu.SemaphoreType.DMA((2,)),
        ],
        compiler_params=pltpu.CompilerParams(
            collective_id=0, has_side_effects=True, vmem_limit_bytes=32 << 20
        ),
    )(in_codes, out_codes, tokens, upstream, wi, wo)


def panel_kernel(in_codes, out_codes, act, gh, wi, wo, parts, lay, inp):
    lay[...] = jnp.zeros_like(lay)
    inp[...] = jnp.zeros_like(inp)

    def outward(k, _):
        i, j, filled = split_code(in_codes, k)

        @pl.when(filled)
        def _():
            inp[i] += dot(gh[j], wi[k], ((1,), (1,)))

        i2, j2, filled2 = split_code(out_codes, k)

        @pl.when(filled2)
        def _():
            lay[i2] += dot(act[j2], wo[k], ((1,), (0,)))

        return 0

    lax.fori_loop(0, wi.shape[0], outward, 0)
    rows, width = parts.shape[-2:]

    def round_up(i, _):
        for t, total in enumerate((lay, inp)):
            full = total[i].astype(BF)
            for core in range(2):
                for lo in range(2):
                    parts[core, i % RING, lo, i // RING, t] = full[
                        lo * rows : (lo + 1) * rows, core * width : (core + 1) * width
                    ]
        return 0

    lax.fori_loop(0, lay.shape[0], round_up, 0)


def panel(in_codes, out_codes, act, gh, wi, wo, rows):
    vmem, smem = specs()
    size = wi.shape[-1]
    total = pltpu.VMEM((2 * RING, 2 * rows, size), F32)
    return pl.pallas_call(
        panel_kernel,
        name="panel",
        out_shape=jax.ShapeDtypeStruct((2, RING, 2, 2, 2, rows, size // 2), BF),
        in_specs=[smem, smem, vmem, vmem, vmem, vmem],
        out_specs=vmem,
        scratch_shapes=[total, total],
        compiler_params=pltpu.CompilerParams(vmem_limit_bytes=32 << 20),
    )(in_codes, out_codes, act, gh, wi, wo)


REDUCE_SENDS = 48


def reduce_kernel(
    in_codes, out_codes, x, act, gh, parts, layer, grad_tokens, grad_in, grad_out,
    pair_buf, y_far, y_buf, z_far, z_buf, end_sum, end_buf,
    send_sems, pair_sems, y_sems, z_sems, end_sems,
):
    at = Place()
    peers = at.peers()
    meet(peers)
    out = Sender(send_sems, peers)
    half = RING // 2
    marks, signs = ("+", "-"), (1, -1)

    def wide(value):
        return value.astype(F32)

    def y_of(dist):
        return lax.rem(at.y + dist + RING, RING)

    def z_of(dist):
        return lax.rem(at.z + dist + RING, RING)

    def share(t, k):
        if t == 0:
            i, j, filled = split_code(in_codes, k)
            product = dot(token_tile(x, 0, i), gh[j], ((0,), (0,)))
        else:
            i, j, filled = split_code(out_codes, k)
            product = dot(act[j], token_tile(x, 1, i), ((0,), (0,)))
        return jnp.where(filled, product, 0.0)

    def chip(y, lo):
        return wide(parts[at.core, y, lo]) + wide(pair_buf[y, lo])

    order = [half] + [sign * dist for dist in range(half - 1, 0, -1) for sign in signs] + [0]
    for dist in order:
        y = y_of(dist)
        out.copy(parts.at[1 - at.core, y], pair_buf.at[y], pair_sems.at[y], "core")
    for d in range(2):
        z_far[d] = share(d, z_of(half)).astype(BF)
        out.copy(z_far.at[d], z_buf.at[d, 0, d], z_sems.at[d, 0, d], "z" + marks[d])
    y = y_of(half)
    out.arrived(pair_buf.at[y], pair_sems.at[y])
    for d in range(2):
        y_far[d] = chip(y, d).astype(BF)
        out.copy(y_far.at[d], y_buf.at[d, 0, d], y_sems.at[d, 0, d], "y" + marks[d])

    def y_hop(step, d, lo):
        y = y_of(signs[d] * (half - step))
        value = chip(y, lo)
        slot = y_buf.at[d, step - 1, lo]
        if step > 1 or lo == d:
            out.arrived(slot, y_sems.at[d, step - 1, lo])
            value = value + wide(slot[...])
        slot[...] = value.astype(BF)
        out.copy(slot, y_buf.at[d, step, lo], y_sems.at[d, step, lo], "y" + marks[d])

    def z_hop(step, d, t):
        value = share(t, z_of(signs[d] * (half - step)))
        slot = z_buf.at[d, step - 1, t]
        if step > 1 or t == d:
            out.arrived(slot, z_sems.at[d, step - 1, t])
            value = value + wide(slot[...])
        slot[...] = value.astype(BF)
        out.copy(slot, z_buf.at[d, step, t], z_sems.at[d, step, t], "z" + marks[d])

    for step in range(1, half):
        for d in range(2):
            y = y_of(signs[d] * (half - step))
            out.arrived(pair_buf.at[y], pair_sems.at[y])
        for n in (1, 0) if step == 1 else (0, 1):
            for d in range(2):
                y_hop(step, d, d if n == 0 else 1 - d)
            for d in range(2):
                z_hop(step, d, d if n == 0 else 1 - d)

    out.arrived(pair_buf.at[at.y], pair_sems.at[at.y])
    own = [share(t, at.z) for t in range(2)]
    for lo in range(2):
        for d in range(2):
            out.arrived(y_buf.at[d, half - 1, lo], y_sems.at[d, half - 1, lo])

    def y_total(lo, hi):
        value = wide(parts[at.core, at.y, lo, hi]) + wide(pair_buf[at.y, lo, hi])
        return value + wide(y_buf[0, half - 1, lo, hi]) + wide(y_buf[1, half - 1, lo, hi])

    ends = (("hi", at.lo, 1 - at.hi), ("diag", 1 - at.lo, 1 - at.hi), ("lo", 1 - at.lo, at.hi))
    for n, (peer, lo, hi) in enumerate(ends):
        end_sum[n] = y_total(lo, hi).astype(BF)
        out.copy(end_sum.at[n], end_buf.at[n], end_sems.at[n], peer)
    for t, result in enumerate((grad_in, grad_out)):
        value = own[t]
        for d in range(2):
            slot = z_buf.at[d, half - 1, t]
            out.arrived(slot, z_sems.at[d, half - 1, t])
            value = value + wide(slot[...])
        result[...] = value.astype(BF)
    total = y_total(at.lo, at.hi)
    for n in (2, 1, 0):
        out.arrived(end_buf.at[n], end_sems.at[n])
        total = total + wide(end_buf[n])
    layer[...] = total[0].astype(BF)
    grad_tokens[...] = total[1].astype(BF)
    out.drain()


def write_kernel(*refs):
    sems = refs[-1]
    count = len(refs) // 2
    copies = [pltpu.make_async_copy(refs[n], refs[count + n], sems.at[n]) for n in range(count)]
    for copy in copies:
        copy.start()
    for copy in copies:
        copy.wait()


def write(*values):
    return pl.pallas_call(
        write_kernel,
        name="write_all",
        out_shape=tuple(jax.ShapeDtypeStruct(v.shape, v.dtype) for v in values),
        in_specs=[pl.BlockSpec(memory_space=pltpu.VMEM)] * len(values),
        out_specs=(pl.BlockSpec(memory_space=pltpu.HBM),) * len(values),
        scratch_shapes=[pltpu.SemaphoreType.DMA((len(values),))],
    )(*values)


def reduce(in_codes, out_codes, x, act, gh, parts):
    vmem, smem = specs()
    rows, width = parts.shape[-2:]
    size = act.shape[-1]
    half = RING // 2
    block, tile = (2, rows, width), (size, size)
    return pl.pallas_call(
        reduce_kernel,
        name="reduce_all",
        out_shape=(
            jax.ShapeDtypeStruct((rows, width), BF),
            jax.ShapeDtypeStruct((rows, width), BF),
            jax.ShapeDtypeStruct(tile, BF),
            jax.ShapeDtypeStruct(tile, BF),
        ),
        in_specs=[smem, smem, vmem, vmem, vmem, vmem],
        out_specs=(vmem,) * 4,
        scratch_shapes=[
            pltpu.VMEM((RING, 2, 2, *block), BF),
            pltpu.VMEM((2, 2, *block), BF),
            pltpu.VMEM((2, half, 2, 2, *block), BF),
            pltpu.VMEM((2, *tile), BF),
            pltpu.VMEM((2, half, 2, *tile), BF),
            pltpu.VMEM((3, *block), BF),
            pltpu.VMEM((3, *block), BF),
            pltpu.SemaphoreType.DMA((REDUCE_SENDS,)),
            pltpu.SemaphoreType.DMA((RING,)),
            pltpu.SemaphoreType.DMA((2, half, 2)),
            pltpu.SemaphoreType.DMA((2, half, 2)),
            pltpu.SemaphoreType.DMA((3,)),
        ],
        compiler_params=pltpu.CompilerParams(
            collective_id=1, has_side_effects=True, vmem_limit_bytes=32 << 20
        ),
    )(in_codes, out_codes, x, act, gh, parts)


def per_device(tokens, upstream, w_in, in_codes, w_out, out_codes):
    in_codes, out_codes = in_codes[0], out_codes[0]
    x, wi, wo, act, gh = gather(in_codes, out_codes, tokens, upstream, w_in[0, 0], w_out[0, 0])
    parts = panel(in_codes, out_codes, act, gh, wi, wo, tokens.shape[0])
    results = reduce(in_codes, out_codes, x, act, gh, parts)
    layer, grad_tokens, grad_in, grad_out = write(*results)
    return layer, grad_tokens, grad_in[None, None], grad_out[None, None]


def solution(mesh):
    placed = (
        P("row", "col"),
        P("row", "col"),
        P("col", "row", None, None),
        P("col", None),
        P("col", "row", None, None),
        P("col", None),
    )
    return jax.shard_map(
        per_device,
        mesh=mesh,
        in_specs=placed,
        out_specs=(
            P("row", "col"),
            P("row", "col"),
            P("col", "row", None, None),
            P("col", "row", None, None),
        ),
        check_vma=False,
    )
```

```python
import jax
import jax.numpy as jnp
from jax import lax
from jax.experimental import pallas as pl
from jax.experimental.pallas import tpu as pltpu
from jax.sharding import PartitionSpec as P

RING = 8
BF, F32 = jnp.bfloat16, jnp.float32


class Place:
    def __init__(self):
        row, col = lax.axis_index("row"), lax.axis_index("col")
        self.row, self.col = row, col
        self.z, self.lo = row // 2, row % 2
        self.hi, self.y, self.core = col // (2 * RING), (col // 2) % RING, col % 2

    def row_at(self, dz=0, lo=None):
        return lax.rem(self.z + dz + RING, RING) * 2 + (self.lo if lo is None else lo)

    def col_at(self, dy=0, hi=None, core=None):
        y = lax.rem(self.y + dy + RING, RING)
        hi = self.hi if hi is None else hi
        return (hi * RING + y) * 2 + (self.core if core is None else core)

    def peers(self):
        return {
            "z+": (self.row_at(1), self.col),
            "z-": (self.row_at(-1), self.col),
            "lo": (self.row_at(0, 1 - self.lo), self.col),
            "y+": (self.row, self.col_at(1)),
            "y-": (self.row, self.col_at(-1)),
            "hi": (self.row, self.col_at(0, 1 - self.hi)),
            "diag": (self.row_at(0, 1 - self.lo), self.col_at(0, 1 - self.hi)),
            "core": (self.row, self.col_at(0, None, 1 - self.core)),
        }


def meet(peers):
    barrier = pltpu.get_barrier_semaphore()
    for device in peers.values():
        pl.semaphore_signal(barrier, inc=1, device_id=device, device_id_type=pl.DeviceIdType.MESH)
    pl.semaphore_wait(barrier, len(peers))


class Sender:
    def __init__(self, sems, peers):
        self.sems, self.peers, self.started = sems, peers, []

    def copy(self, src, dst, recv_sem, peer):
        copy = pltpu.make_async_remote_copy(
            src_ref=src,
            dst_ref=dst,
            send_sem=self.sems.at[len(self.started)],
            recv_sem=recv_sem,
            device_id=self.peers[peer],
            device_id_type=pl.DeviceIdType.MESH,
        )
        copy.start()
        self.started.append(copy)

    def arrived(self, dst, recv_sem):
        pltpu.make_async_remote_copy(
            src_ref=dst,
            dst_ref=dst,
            send_sem=self.sems.at[0],
            recv_sem=recv_sem,
            device_id=self.peers["core"],
            device_id_type=pl.DeviceIdType.MESH,
        ).wait_recv()

    def drain(self):
        for copy in self.started:
            copy.wait_send()


def dot(a, b, contract):
    return lax.dot_general(a, b, (contract, ((), ())), preferred_element_type=F32)


def split_code(ref, k):
    code = ref[2 * k + lax.axis_index("row") % 2]
    clipped = jnp.maximum(code, 0)
    return clipped // 2, clipped % 2, code >= 0


def token_tile(x, which, i):
    halves = [jnp.concatenate([x[lo, 2 * i, which], x[lo, 2 * i + 1, which]], axis=1) for lo in range(2)]
    return jnp.concatenate(halves, axis=0)


SENDS = 144


def whole_kernel(
    in_codes, out_codes, tokens, upstream, wi_ref, wo_ref, layer, grad_tokens, grad_in, grad_out,
    xg, wig, wog, hid, gact, mine, theirs, act, gh, slot_of,
    parts, pair_buf, y_far, y_buf, z_far, z_buf, end_sum, end_buf,
    send_sems, x_sems, w_sems, own_sems, swap_sems, pair_sems, y_sems, z_sems, end_sems,
):
    at = Place()
    peers = at.peers()
    x_own = xg.at[at.lo, at.col]
    own = [
        pltpu.make_async_copy(tokens, x_own.at[0], own_sems.at[0]),
        pltpu.make_async_copy(upstream, x_own.at[1], own_sems.at[1]),
        pltpu.make_async_copy(wi_ref, wig.at[at.z], own_sems.at[2]),
        pltpu.make_async_copy(wo_ref, wog.at[at.z], own_sems.at[3]),
    ]
    for copy in own:
        copy.start()
    meet(peers)
    out = Sender(send_sems, peers)
    for copy in own:
        copy.wait()
    held = (wig, wog)

    def x_send(lo, col, *to):
        for peer in to:
            out.copy(xg.at[lo, col], xg.at[lo, col], x_sems.at[lo, col], peer)

    def x_pass(lo, col, *to):
        out.arrived(xg.at[lo, col], x_sems.at[lo, col])
        x_send(lo, col, *to)

    def w_send(t, z, *to):
        for peer in to:
            out.copy(held[t].at[z], held[t].at[z], w_sems.at[t, z], peer)

    def w_pass(t, z, *to):
        out.arrived(held[t].at[z], w_sems.at[t, z])
        w_send(t, z, *to)

    x_send(at.lo, at.col, "y+", "y-", "lo", "diag", "hi")
    for t in range(2):
        w_send(t, at.z, "z+", "z-")
    x_send(at.lo, at.col, "core")
    x_pass(1 - at.lo, at.col, "y+", "y-", "core")
    x_pass(at.lo, at.col_at(0, 1 - at.hi), "y+", "y-", "core")
    x_pass(1 - at.lo, at.col_at(0, 1 - at.hi), "y+", "y-", "core")
    half = RING // 2
    flows = ((-1, "+"), (1, "-"))
    kinds = ((at.lo, at.hi), (1 - at.lo, at.hi), (at.lo, 1 - at.hi), (1 - at.lo, 1 - at.hi))
    for step in range(1, half + 1):
        for n, (lo, hi) in enumerate(kinds):
            for d, (sign, mark) in enumerate(flows):
                if step == half and n % 2 != d:
                    continue
                onward = step < half - 1 or (step == half - 1 and n % 2 == d)
                x_pass(lo, at.col_at(sign * step, hi), *(("y" + mark,) if onward else ()), "core")
            if n % 2 == 1:
                continue
            t = n // 2
            for d, (sign, mark) in enumerate(flows):
                if step == half and t != d:
                    continue
                onward = step < half - 1 or (step == half - 1 and t == d)
                w_pass(t, lax.rem(at.z + sign * step + RING, RING), *(("z" + mark,) if onward else ()))
    for step in range(RING):
        for hi in range(2):
            for lo in range(2):
                col = at.col_at(step, hi, 1 - at.core)
                out.arrived(xg.at[lo, col], x_sems.at[lo, col])

    hid[...] = jnp.zeros_like(hid)
    gact[...] = jnp.zeros_like(gact)

    def inward(codes, which, weights, total, contract):
        def one(k, _):
            i, j, filled = split_code(codes, k)
            product = dot(token_tile(xg, which, i), weights[k], contract)
            for col in range(2):
                total[col] += jnp.where(jnp.logical_and(filled, j == col), product, 0.0)
            return 0

        lax.fori_loop(0, RING, one, 0, unroll=True)
        mine[which] = total[...].astype(BF)
        out.copy(mine.at[which], theirs.at[which], swap_sems.at[which], "lo")

    inward(in_codes, 0, wig, hid, ((1,), (0,)))
    inward(out_codes, 1, wog, gact, ((1,), (1,)))

    def slot_at(code, _):
        for t, codes in enumerate((in_codes, out_codes)):
            slot = jnp.int32(-1)
            for k in range(RING):
                slot = jnp.where(codes[2 * k + at.lo] == code, k, slot)
            slot_of[t, code] = slot
        return 0

    lax.fori_loop(0, 4 * RING, slot_at, 0)

    marks, signs = ("+", "-"), (1, -1)
    size = hid.shape[-1]
    width = size // 2

    def wide(value):
        return value.astype(F32)

    def y_of(dist):
        return lax.rem(at.y + dist + RING, RING)

    def z_of(dist):
        return lax.rem(at.z + dist + RING, RING)

    def share(t, k):
        if t == 0:
            i, j, filled = split_code(in_codes, k)
            product = dot(token_tile(xg, 0, i), gh[j], ((0,), (0,)))
        else:
            i, j, filled = split_code(out_codes, k)
            product = dot(act[j], token_tile(xg, 1, i), ((0,), (0,)))
        return jnp.where(filled, product, 0.0)

    order = [half] + [sign * dist for dist in range(half - 1, 0, -1) for sign in signs] + [0]

    def make(t):
        left, weights, contract = ((act, wog, ((1,), (0,))), (gh, wig, ((1,), (1,))))[t]
        for dist in order:
            y = y_of(dist)
            for hi in range(2):
                full = jnp.zeros((size, size), F32)
                for j in range(2):
                    slot = slot_of[1 - t, 2 * (hi * RING + y) + j]
                    product = dot(left[j], weights[jnp.maximum(slot, 0)], contract)
                    full = full + jnp.where(slot >= 0, product, 0.0)
                full = full.astype(BF)
                for core in range(2):
                    for lo in range(2):
                        parts[core, t, y, lo, hi] = full[
                            lo * width : (lo + 1) * width, core * width : (core + 1) * width
                        ]
            out.copy(parts.at[1 - at.core, t, y], pair_buf.at[t, y], pair_sems.at[t, y], "core")

    def z_start(t):
        z_far[t] = share(t, z_of(half)).astype(BF)
        out.copy(z_far.at[t], z_buf.at[t, 0, t], z_sems.at[t, 0, t], "z" + marks[t])

    def chip(t, y):
        return wide(parts[at.core, t, y]) + wide(pair_buf[t, y])

    def paired(t, y):
        out.arrived(pair_buf.at[t, y], pair_sems.at[t, y])

    def y_start(t):
        y = y_of(half)
        paired(t, y)
        y_far[t] = chip(t, y).astype(BF)
        for d in range(2):
            out.copy(y_far.at[t, d], y_buf.at[d, 0, t, d], y_sems.at[d, 0, t], "y" + marks[d])

    def y_hop(step, d, t):
        y = y_of(signs[d] * (half - step))
        paired(t, y)
        value = chip(t, y)
        slot = y_buf.at[d, step - 1, t]
        if step == 1:
            out.arrived(slot.at[d], y_sems.at[d, 0, t])
            slot[d] = (value[d] + wide(slot[d])).astype(BF)
            slot[1 - d] = value[1 - d].astype(BF)
        else:
            out.arrived(slot, y_sems.at[d, step - 1, t])
            slot[...] = (value + wide(slot[...])).astype(BF)
        out.copy(slot, y_buf.at[d, step, t], y_sems.at[d, step, t], "y" + marks[d])

    def z_hop(step, d, t):
        value = share(t, z_of(signs[d] * (half - step)))
        slot = z_buf.at[d, step - 1, t]
        if step > 1 or t == d:
            out.arrived(slot, z_sems.at[d, step - 1, t])
            value = value + wide(slot[...])
        slot[...] = value.astype(BF)
        out.copy(slot, z_buf.at[d, step, t], z_sems.at[d, step, t], "z" + marks[d])

    out.arrived(theirs.at[0], swap_sems.at[0])
    for j in range(2):
        h = hid[j] + wide(theirs[0, j])
        s = jax.nn.sigmoid(h)
        act[j] = (h * s).astype(BF)
        hid[j] = s * (1.0 + h * (1.0 - s))
    z_start(1)
    make(0)
    y_start(0)
    out.arrived(theirs.at[1], swap_sems.at[1])
    for j in range(2):
        gh[j] = ((gact[j] + wide(theirs[1, j])) * hid[j]).astype(BF)
    z_start(0)
    z_hop(1, 0, 1)
    make(1)
    y_start(1)
    for step in range(1, half):
        for t in range(2):
            for d in range(2):
                y_hop(step, d, t)
            for d in range(2):
                if (step, d, t) != (1, 0, 0):
                    z_hop(step, d, 1 - t)

    for t in range(2):
        paired(t, at.y)
    own = [share(t, at.z) for t in range(2)]
    for t in range(2):
        for d in range(2):
            out.arrived(y_buf.at[d, half - 1, t], y_sems.at[d, half - 1, t])

    def y_total(t, lo, hi):
        value = wide(parts[at.core, t, at.y, lo, hi]) + wide(pair_buf[t, at.y, lo, hi])
        return value + wide(y_buf[0, half - 1, t, lo, hi]) + wide(y_buf[1, half - 1, t, lo, hi])

    ends = (("hi", at.lo, 1 - at.hi), ("diag", 1 - at.lo, 1 - at.hi), ("lo", 1 - at.lo, at.hi))
    for n, (peer, lo, hi) in enumerate(ends):
        for t in range(2):
            end_sum[n, t] = y_total(t, lo, hi).astype(BF)
        out.copy(end_sum.at[n], end_buf.at[n], end_sems.at[n], peer)
    for t, result in enumerate((grad_in, grad_out)):
        value = own[t]
        for d in range(2):
            slot = z_buf.at[d, half - 1, t]
            out.arrived(slot, z_sems.at[d, half - 1, t])
            value = value + wide(slot[...])
        result[...] = value.astype(BF)
    for n in range(3):
        out.arrived(end_buf.at[n], end_sems.at[n])
    for t, result in enumerate((layer, grad_tokens)):
        total = y_total(t, at.lo, at.hi)
        for n in range(3):
            total = total + wide(end_buf[n, t])
        result[...] = total.astype(BF)
    out.drain()


def whole(in_codes, out_codes, tokens, upstream, wi, wo):
    vmem, smem = pl.BlockSpec(memory_space=pltpu.VMEM), pl.BlockSpec(memory_space=pltpu.SMEM)
    tile, block = wi.shape, tokens.shape
    half = RING // 2
    pair = (2, 2 * block[0], tile[1])
    chunk = (2, 2, *block)
    dma = pltpu.SemaphoreType.DMA
    return pl.pallas_call(
        whole_kernel,
        name="whole_layer",
        out_shape=tuple(jax.ShapeDtypeStruct(shape, BF) for shape in (block, block, tile, tile)),
        in_specs=[smem, smem] + [pl.BlockSpec(memory_space=pl.ANY)] * 4,
        out_specs=(vmem,) * 4,
        scratch_shapes=[
            pltpu.VMEM((2, 4 * RING, 2, *block), BF),
            pltpu.VMEM((RING, *tile), BF),
            pltpu.VMEM((RING, *tile), BF),
            pltpu.VMEM(pair, F32),
            pltpu.VMEM(pair, F32),
            pltpu.VMEM((2, *pair), BF),
            pltpu.VMEM((2, *pair), BF),
            pltpu.VMEM(pair, BF),
            pltpu.VMEM(pair, BF),
            pltpu.SMEM((2, 4 * RING), jnp.int32),
            pltpu.VMEM((2, 2, RING, *chunk), BF),
            pltpu.VMEM((2, RING, *chunk), BF),
            pltpu.VMEM((2, *chunk), BF),
            pltpu.VMEM((2, half, 2, *chunk), BF),
            pltpu.VMEM((2, *tile), BF),
            pltpu.VMEM((2, half, 2, *tile), BF),
            pltpu.VMEM((3, 2, *block), BF),
            pltpu.VMEM((3, 2, *block), BF),
            dma((SENDS,)),
            dma((2, 4 * RING)),
            dma((2, RING)),
            dma((4,)),
            dma((2,)),
            dma((2, RING)),
            dma((2, half, 2)),
            dma((2, half, 2)),
            dma((3,)),
        ],
        compiler_params=pltpu.CompilerParams(
            collective_id=0, has_side_effects=True, vmem_limit_bytes=61 << 20
        ),
    )(in_codes, out_codes, tokens, upstream, wi, wo)


def per_device(tokens, upstream, w_in, in_codes, w_out, out_codes):
    layer, grad_tokens, grad_in, grad_out = whole(
        in_codes[0], out_codes[0], tokens, upstream, w_in[0, 0], w_out[0, 0]
    )
    return layer, grad_tokens, grad_in[None, None], grad_out[None, None]


def solution(mesh):
    placed = (
        P("row", "col"),
        P("row", "col"),
        P("col", "row", None, None),
        P("col", None),
        P("col", "row", None, None),
        P("col", None),
    )
    return jax.shard_map(
        per_device,
        mesh=mesh,
        in_specs=placed,
        out_specs=(
            P("row", "col"),
            P("row", "col"),
            P("col", "row", None, None),
            P("col", "row", None, None),
        ),
        check_vma=False,
    )
```

```python
import jax
import jax.numpy as jnp
from jax import lax
from jax.experimental import pallas as pl
from jax.experimental.pallas import tpu as pltpu
from jax.sharding import PartitionSpec as P

RING = 8
BF, F32 = jnp.bfloat16, jnp.float32


class Place:
    def __init__(self):
        row, col = lax.axis_index("row"), lax.axis_index("col")
        self.row, self.col = row, col
        self.z, self.lo = row // 2, row % 2
        self.hi, self.y, self.core = col // (2 * RING), (col // 2) % RING, col % 2

    def row_at(self, dz=0, lo=None):
        return lax.rem(self.z + dz + RING, RING) * 2 + (self.lo if lo is None else lo)

    def col_at(self, dy=0, hi=None, core=None):
        y = lax.rem(self.y + dy + RING, RING)
        hi = self.hi if hi is None else hi
        return (hi * RING + y) * 2 + (self.core if core is None else core)

    def peers(self):
        return {
            "z+": (self.row_at(1), self.col),
            "z-": (self.row_at(-1), self.col),
            "lo": (self.row_at(0, 1 - self.lo), self.col),
            "y+": (self.row, self.col_at(1)),
            "y-": (self.row, self.col_at(-1)),
            "hi": (self.row, self.col_at(0, 1 - self.hi)),
            "diag": (self.row_at(0, 1 - self.lo), self.col_at(0, 1 - self.hi)),
            "core": (self.row, self.col_at(0, None, 1 - self.core)),
        }


def meet(peers):
    barrier = pltpu.get_barrier_semaphore()
    for device in peers.values():
        pl.semaphore_signal(barrier, inc=1, device_id=device, device_id_type=pl.DeviceIdType.MESH)
    pl.semaphore_wait(barrier, len(peers))


class Sender:
    def __init__(self, sems, peers):
        self.sems, self.peers, self.started = sems, peers, []

    def copy(self, src, dst, recv_sem, peer):
        copy = pltpu.make_async_remote_copy(
            src_ref=src,
            dst_ref=dst,
            send_sem=self.sems.at[len(self.started)],
            recv_sem=recv_sem,
            device_id=self.peers[peer],
            device_id_type=pl.DeviceIdType.MESH,
        )
        copy.start()
        self.started.append(copy)

    def arrived(self, dst, recv_sem):
        pltpu.make_async_remote_copy(
            src_ref=dst,
            dst_ref=dst,
            send_sem=self.sems.at[0],
            recv_sem=recv_sem,
            device_id=self.peers["core"],
            device_id_type=pl.DeviceIdType.MESH,
        ).wait_recv()

    def drain(self):
        for copy in self.started:
            copy.wait_send()


def dot(a, b, contract):
    return lax.dot_general(a, b, (contract, ((), ())), preferred_element_type=F32)


def split_code(ref, k):
    code = ref[2 * k + lax.axis_index("row") % 2]
    clipped = jnp.maximum(code, 0)
    return clipped // 2, clipped % 2, code >= 0


def token_tile(x, which, i):
    halves = [jnp.concatenate([x[lo, 2 * i, which], x[lo, 2 * i + 1, which]], axis=1) for lo in range(2)]
    return jnp.concatenate(halves, axis=0)


SENDS = 144


def whole_kernel(
    in_codes, out_codes, tokens, upstream, wi_ref, wo_ref, sums, grads,
    xg, wig, wog, hid, gact, mine, theirs, act, gh, slot_of,
    parts, pair_buf, y_far, y_buf, z_far, z_buf, end_sum, end_buf,
    send_sems, x_sems, w_sems, own_sems, swap_sems, pair_sems, y_sems, z_sems, end_sems,
):
    at = Place()
    peers = at.peers()
    x_own = xg.at[at.lo, at.col]
    own = [
        pltpu.make_async_copy(tokens, x_own.at[0], own_sems.at[0]),
        pltpu.make_async_copy(upstream, x_own.at[1], own_sems.at[1]),
        pltpu.make_async_copy(wi_ref, wig.at[at.z], own_sems.at[2]),
        pltpu.make_async_copy(wo_ref, wog.at[at.z], own_sems.at[3]),
    ]
    for copy in own:
        copy.start()
    meet(peers)
    out = Sender(send_sems, peers)
    for copy in own:
        copy.wait()
    held = (wig, wog)

    def x_send(lo, col, *to):
        for peer in to:
            out.copy(xg.at[lo, col], xg.at[lo, col], x_sems.at[lo, col], peer)

    def x_pass(lo, col, *to):
        out.arrived(xg.at[lo, col], x_sems.at[lo, col])
        x_send(lo, col, *to)

    def w_send(t, z, *to):
        for peer in to:
            out.copy(held[t].at[z], held[t].at[z], w_sems.at[t, z], peer)

    def w_pass(t, z, *to):
        out.arrived(held[t].at[z], w_sems.at[t, z])
        w_send(t, z, *to)

    x_send(at.lo, at.col, "y+", "y-", "lo", "diag", "hi")
    for t in range(2):
        w_send(t, at.z, "z+", "z-")
    x_send(at.lo, at.col, "core")
    x_pass(1 - at.lo, at.col, "y+", "y-", "core")
    x_pass(at.lo, at.col_at(0, 1 - at.hi), "y+", "y-", "core")
    x_pass(1 - at.lo, at.col_at(0, 1 - at.hi), "y+", "y-", "core")
    half = RING // 2
    flows = ((-1, "+"), (1, "-"))
    kinds = ((at.lo, at.hi), (1 - at.lo, at.hi), (at.lo, 1 - at.hi), (1 - at.lo, 1 - at.hi))
    for step in range(1, half + 1):
        for n, (lo, hi) in enumerate(kinds):
            for d, (sign, mark) in enumerate(flows):
                if step == half and n % 2 != d:
                    continue
                onward = step < half - 1 or (step == half - 1 and n % 2 == d)
                x_pass(lo, at.col_at(sign * step, hi), *(("y" + mark,) if onward else ()), "core")
            if n % 2 == 1:
                continue
            t = n // 2
            for d, (sign, mark) in enumerate(flows):
                if step == half and (t != d or t == 1):
                    continue
                onward = step < half - 1 or (step == half - 1 and t == d)
                w_pass(t, lax.rem(at.z + sign * step + RING, RING), *(("z" + mark,) if onward else ()))
    for step in range(RING):
        for hi in range(2):
            for lo in range(2):
                col = at.col_at(step, hi, 1 - at.core)
                out.arrived(xg.at[lo, col], x_sems.at[lo, col])

    hid[...] = jnp.zeros_like(hid)
    gact[...] = jnp.zeros_like(gact)

    def inward(codes, which, weights, total, contract):
        def one(k, _):
            i, j, filled = split_code(codes, k)
            product = dot(token_tile(xg, which, i), weights[k], contract)
            for col in range(2):
                total[col] += jnp.where(jnp.logical_and(filled, j == col), product, 0.0)
            return 0

        lax.fori_loop(0, RING, one, 0, unroll=True)
        mine[which] = total[...].astype(BF)
        out.copy(mine.at[which], theirs.at[which], swap_sems.at[which], "lo")

    inward(in_codes, 0, wig, hid, ((1,), (0,)))
    w_pass(1, lax.rem(at.z + half, RING))
    inward(out_codes, 1, wog, gact, ((1,), (1,)))

    def slot_at(code, _):
        for t, codes in enumerate((in_codes, out_codes)):
            slot = jnp.int32(-1)
            for k in range(RING):
                slot = jnp.where(codes[2 * k + at.lo] == code, k, slot)
            slot_of[t, code] = slot
        return 0

    lax.fori_loop(0, 4 * RING, slot_at, 0)

    marks, signs = ("+", "-"), (1, -1)
    size = hid.shape[-1]
    width = size // 2

    def wide(value):
        return value.astype(F32)

    def y_of(dist):
        return lax.rem(at.y + dist + RING, RING)

    def z_of(dist):
        return lax.rem(at.z + dist + RING, RING)

    def share(t, k):
        if t == 0:
            i, j, filled = split_code(in_codes, k)
            product = dot(token_tile(xg, 0, i), gh[j], ((0,), (0,)))
        else:
            i, j, filled = split_code(out_codes, k)
            product = dot(act[j], token_tile(xg, 1, i), ((0,), (0,)))
        return jnp.where(filled, product, 0.0)

    order = [half] + [sign * dist for dist in range(half - 1, 0, -1) for sign in signs] + [0]

    def make(t):
        left, weights, contract = ((act, wog, ((1,), (0,))), (gh, wig, ((1,), (1,))))[t]
        for dist in order:
            y = y_of(dist)
            for hi in range(2):
                full = jnp.zeros((size, size), F32)
                for j in range(2):
                    slot = slot_of[1 - t, 2 * (hi * RING + y) + j]
                    product = dot(left[j], weights[jnp.maximum(slot, 0)], contract)
                    full = full + jnp.where(slot >= 0, product, 0.0)
                full = full.astype(BF)
                for core in range(2):
                    for lo in range(2):
                        parts[core, t, y, lo, hi] = full[
                            lo * width : (lo + 1) * width, core * width : (core + 1) * width
                        ]
            out.copy(parts.at[1 - at.core, t, y], pair_buf.at[t, y], pair_sems.at[t, y], "core")

    def z_start(t):
        z_far[t] = share(t, z_of(half)).astype(BF)
        out.copy(z_far.at[t], z_buf.at[t, 0, t], z_sems.at[t, 0, t], "z" + marks[t])

    def chip(t, y):
        return wide(parts[at.core, t, y]) + wide(pair_buf[t, y])

    def paired(t, y):
        out.arrived(pair_buf.at[t, y], pair_sems.at[t, y])

    def y_start(t):
        y = y_of(half)
        paired(t, y)
        y_far[t] = chip(t, y).astype(BF)
        for d in range(2):
            out.copy(y_far.at[t, d], y_buf.at[d, 0, t, d], y_sems.at[d, 0, t], "y" + marks[d])

    def y_hop(step, d, t):
        y = y_of(signs[d] * (half - step))
        paired(t, y)
        value = chip(t, y)
        slot = y_buf.at[d, step - 1, t]
        if step == 1:
            out.arrived(slot.at[d], y_sems.at[d, 0, t])
            slot[d] = (value[d] + wide(slot[d])).astype(BF)
            slot[1 - d] = value[1 - d].astype(BF)
        else:
            out.arrived(slot, y_sems.at[d, step - 1, t])
            slot[...] = (value + wide(slot[...])).astype(BF)
        out.copy(slot, y_buf.at[d, step, t], y_sems.at[d, step, t], "y" + marks[d])

    def z_hop(step, d, t):
        value = share(t, z_of(signs[d] * (half - step)))
        slot = z_buf.at[d, step - 1, t]
        if step > 1 or t == d:
            out.arrived(slot, z_sems.at[d, step - 1, t])
            value = value + wide(slot[...])
        slot[...] = value.astype(BF)
        out.copy(slot, z_buf.at[d, step, t], z_sems.at[d, step, t], "z" + marks[d])

    out.arrived(theirs.at[0], swap_sems.at[0])
    for j in range(2):
        h = hid[j] + wide(theirs[0, j])
        s = jax.nn.sigmoid(h)
        act[j] = (h * s).astype(BF)
        hid[j] = s * (1.0 + h * (1.0 - s))
    z_start(1)
    make(0)
    y_start(0)
    out.arrived(theirs.at[1], swap_sems.at[1])
    for j in range(2):
        gh[j] = ((gact[j] + wide(theirs[1, j])) * hid[j]).astype(BF)
    z_start(0)
    z_hop(1, 0, 1)
    make(1)
    y_start(1)
    for step in range(1, half):
        for t in range(2):
            for d in range(2):
                y_hop(step, d, t)
            for d in range(2):
                if (step, d, t) != (1, 0, 0):
                    z_hop(step, d, 1 - t)

    for t in range(2):
        paired(t, at.y)
    own = [share(t, at.z) for t in range(2)]
    for t in range(2):
        for d in range(2):
            out.arrived(y_buf.at[d, half - 1, t], y_sems.at[d, half - 1, t])

    def y_total(t, lo, hi):
        value = wide(parts[at.core, t, at.y, lo, hi]) + wide(pair_buf[t, at.y, lo, hi])
        return value + wide(y_buf[0, half - 1, t, lo, hi]) + wide(y_buf[1, half - 1, t, lo, hi])

    ends = (("hi", at.lo, 1 - at.hi), ("diag", 1 - at.lo, 1 - at.hi), ("lo", 1 - at.lo, at.hi))
    for n, (peer, lo, hi) in enumerate(ends):
        for t in range(2):
            end_sum[n, t] = y_total(t, lo, hi).astype(BF)
        out.copy(end_sum.at[n], end_buf.at[n], end_sems.at[n], peer)
    for t in range(2):
        value = own[t]
        for d in range(2):
            slot = z_buf.at[d, half - 1, t]
            out.arrived(slot, z_sems.at[d, half - 1, t])
            value = value + wide(slot[...])
        grads[t] = value.astype(BF)
    for n in range(3):
        out.arrived(end_buf.at[n], end_sems.at[n])
    for t in range(2):
        total = y_total(t, at.lo, at.hi)
        for n in range(3):
            total = total + wide(end_buf[n, t])
        sums[t] = total.astype(BF)
    out.drain()


def whole(in_codes, out_codes, tokens, upstream, wi, wo):
    vmem, smem = pl.BlockSpec(memory_space=pltpu.VMEM), pl.BlockSpec(memory_space=pltpu.SMEM)
    tile, block = wi.shape, tokens.shape
    half = RING // 2
    pair = (2, 2 * block[0], tile[1])
    chunk = (2, 2, *block)
    dma = pltpu.SemaphoreType.DMA
    return pl.pallas_call(
        whole_kernel,
        name="whole_layer",
        out_shape=tuple(jax.ShapeDtypeStruct(shape, BF) for shape in ((2, *block), (2, *tile))),
        in_specs=[smem, smem] + [pl.BlockSpec(memory_space=pl.ANY)] * 4,
        out_specs=(vmem,) * 2,
        scratch_shapes=[
            pltpu.VMEM((2, 4 * RING, 2, *block), BF),
            pltpu.VMEM((RING, *tile), BF),
            pltpu.VMEM((RING, *tile), BF),
            pltpu.VMEM(pair, F32),
            pltpu.VMEM(pair, F32),
            pltpu.VMEM((2, *pair), BF),
            pltpu.VMEM((2, *pair), BF),
            pltpu.VMEM(pair, BF),
            pltpu.VMEM(pair, BF),
            pltpu.SMEM((2, 4 * RING), jnp.int32),
            pltpu.VMEM((2, 2, RING, *chunk), BF),
            pltpu.VMEM((2, RING, *chunk), BF),
            pltpu.VMEM((2, *chunk), BF),
            pltpu.VMEM((2, half, 2, *chunk), BF),
            pltpu.VMEM((2, *tile), BF),
            pltpu.VMEM((2, half, 2, *tile), BF),
            pltpu.VMEM((3, 2, *block), BF),
            pltpu.VMEM((3, 2, *block), BF),
            dma((SENDS,)),
            dma((2, 4 * RING)),
            dma((2, RING)),
            dma((4,)),
            dma((2,)),
            dma((2, RING)),
            dma((2, half, 2)),
            dma((2, half, 2)),
            dma((3,)),
        ],
        compiler_params=pltpu.CompilerParams(
            collective_id=0, has_side_effects=True, vmem_limit_bytes=61 << 20
        ),
    )(in_codes, out_codes, tokens, upstream, wi, wo)


def per_device(tokens, upstream, w_in, in_codes, w_out, out_codes):
    sums, grads = whole(
        in_codes[0], out_codes[0], tokens, upstream, w_in[0, 0], w_out[0, 0]
    )
    return sums[0], sums[1], grads[0][None, None], grads[1][None, None]


def solution(mesh):
    placed = (
        P("row", "col"),
        P("row", "col"),
        P("col", "row", None, None),
        P("col", None),
        P("col", "row", None, None),
        P("col", None),
    )
    return jax.shard_map(
        per_device,
        mesh=mesh,
        in_specs=placed,
        out_specs=(
            P("row", "col"),
            P("row", "col"),
            P("col", "row", None, None),
            P("col", "row", None, None),
        ),
        check_vma=False,
    )
```
